1024 devices in a mesh: sec: 4 (over x), gx: 64 (over z_lo, y), gz: 4 (over z_hi, core).
Axes of the slice: x: 4, y: 4, z: 32 (z_hi: 2, z_lo: 16; z = z_hi * 16 + z_lo), core: 2. Of those that a mesh axis runs over, the one named last changes fastest.
Arguments:
- fields: float32 [4, 5, 8192, 512], P('sec', None, 'gx', 'gz'), may hold values from -6 to 6
- media: float32 [4, 3, 8192, 512], P('sec', None, 'gx', 'gz'), may hold values from 0.5 to 2
- plane_rows: int32 [32], replicated, may hold values from 0 to 511, as said below
- box_offset: int32 [3], replicated, may hold values from 0 to 256
Outputs:
- evolved: float32 [4, 5, 8192, 512], P('sec', None, 'gx', 'gz')
The draws below stay inside these ranges and needn't reach their ends.
Inputs may be any that keep to these rules, and one draw needn't show every extreme that they name: `plane_rows`: entries 8 * j to 8 * j + 7 are distinct rows of the j-th depth block of 128 rows; row 0 and row 511 are always among them.
All inputs are finite; a program needn't handle non-finite values.
Results may differ from the reference program's by a relative error of at most 0.00013.
Values sent between devices are 32-bit elements; how exact they have to be, the bound alone decides.
A program may use at most 32 MiB of HBM per device.

```python
import math
import jax
import jax.numpy as jnp
from jax import lax

CZ = 128
RADIUS = 4
STEPS = 5
NPD = 8
NX = 8192
NZ = 512
NP = 32
FAR = 3
N_SEC = 4
N_GZ = 4


def draw_plane_rows(key, part):
    scores = jax.random.randint(key, (N_GZ, CZ), 0, 4096)
    blocks = lax.broadcasted_iota(jnp.int32, (N_GZ, CZ), 0)
    columns = lax.broadcasted_iota(jnp.int32, (N_GZ, CZ), 1)
    pinned = (blocks == 0) & (columns == 0) | (blocks == N_GZ - 1) & (columns == CZ - 1)
    ranked = scores * CZ + columns + jnp.where(pinned, 8192 * CZ, 0)
    ranked_values, picked = lax.top_k(ranked, NPD)
    return (picked + blocks[:, :NPD] * CZ).reshape(NP).astype(jnp.int32)


def shard_levels(own_key, extent, split, least, high):
    factor_of, own = 1.0, jax.random.fold_in(own_key, 6)
    for position, shards_of in split:
        heights = jnp.exp(jax.random.uniform(jax.random.fold_in(own, position), (shards_of,), jnp.float32, least / len(split), high / len(split)))
        factor_of = factor_of * jnp.repeat(heights, extent[position] // shards_of).reshape([-1 if axis == position else 1 for axis in range(len(extent))])
    return factor_of


def noise(own_key, extent, width, reach, cuts=(), kind=jnp.bfloat16):
    factor_of = shard_levels(own_key, extent, cuts, -0.22, 0.18) if cuts else 1.0
    values = jax.random.normal(own_key, extent, jnp.float32) * width * factor_of
    return jnp.minimum(jnp.maximum(values, -reach), reach).astype(kind)


def setup_inputs(seed: int = 0) -> dict:
    arg_keys = jax.random.split(jax.random.key(seed), 5)
    return {
        "fields": noise(arg_keys[0], (N_SEC, 5, NX, NZ), 1.0, 6.0, ((0, 4), (2, 64), (3, 4)), jnp.float32),
        "media": jnp.clip(jnp.exp(math.log(2.0) - 1.3862944 * jax.random.uniform(arg_keys[1], (N_SEC, 3, NX, NZ), jnp.float32) ** shard_levels(arg_keys[1], (N_SEC, 3, NX, NZ), ((0, 4), (2, 64), (3, 4)), -0.2, 0.2)), 0.5, 2.0),
        "plane_rows": draw_plane_rows(jax.random.fold_in(arg_keys[4], 71), 0),
        "box_offset": jax.random.randint(arg_keys[3], (FAR,), 0, NZ // 2 + 1).astype(jnp.int32),
    }


STENCIL = (0.8, -0.2, 4.0 / 105.0, -1.0 / 280.0)
TIME_STEP = 0.2
COUPLING = 0.5
RELAXATION = (0.9, 0.5)
MEMORY_WEIGHT = (0.15, 0.1)


def along_x(padded, anchor, count_x, count_z):
    summed = jnp.zeros(padded.shape[:-2] + (count_x, count_z), jnp.float32)
    for offset, stencil_tap in enumerate(STENCIL, 1):
        forward = padded[..., anchor + offset:anchor + offset + count_x, anchor:anchor + count_z]
        backward = padded[..., anchor - offset:anchor - offset + count_x, anchor:anchor + count_z]
        summed = summed + stencil_tap * (forward - backward)
    return summed


def along_z(padded, anchor, count_x, count_z):
    summed = jnp.zeros(padded.shape[:-2] + (count_x, count_z), jnp.float32)
    for offset, stencil_tap in enumerate(STENCIL, 1):
        forward = padded[..., anchor:anchor + count_x, anchor + offset:anchor + offset + count_z]
        backward = padded[..., anchor:anchor + count_x, anchor - offset:anchor - offset + count_z]
        summed = summed + stencil_tap * (forward - backward)
    return summed


def velocity_elastic(velocity, stresses, buoyancy, anchor, count_x, count_z):
    updated_x = velocity[0] + TIME_STEP * buoyancy * (along_x(stresses[0], anchor, count_x, count_z) + along_z(stresses[2], anchor, count_x, count_z))
    updated_z = velocity[1] + TIME_STEP * buoyancy * (along_x(stresses[2], anchor, count_x, count_z) + along_z(stresses[1], anchor, count_x, count_z))
    return jnp.stack([updated_x, updated_z])


def velocity_acoustic(velocity, stresses, buoyancy, anchor, count_x, count_z):
    updated_x = velocity[0] - TIME_STEP * buoyancy * along_x(stresses[0], anchor, count_x, count_z)
    updated_z = velocity[1] - TIME_STEP * buoyancy * along_z(stresses[0], anchor, count_x, count_z)
    return jnp.stack([updated_x, updated_z])


def stress_elastic(stresses, velocity_pad, material, anchor, count_x, count_z):
    strain_x = along_x(velocity_pad[0], anchor, count_x, count_z)
    strain_z = along_z(velocity_pad[1], anchor, count_x, count_z)
    strain_shear = along_z(velocity_pad[0], anchor, count_x, count_z) + along_x(velocity_pad[1], anchor, count_x, count_z)
    lame_first = material[1]
    shear_modulus = material[2]
    normal_x = stresses[0] + TIME_STEP * ((lame_first + 2.0 * shear_modulus) * strain_x + lame_first * strain_z)
    normal_z = stresses[1] + TIME_STEP * (lame_first * strain_x + (lame_first + 2.0 * shear_modulus) * strain_z)
    shear_new = stresses[2] + TIME_STEP * shear_modulus * strain_shear
    return jnp.stack([normal_x, normal_z, shear_new])


def stress_acoustic(stresses, velocity_pad, material, anchor, count_x, count_z):
    divergence = along_x(velocity_pad[0], anchor, count_x, count_z) + along_z(velocity_pad[1], anchor, count_x, count_z)
    loading = material[1] * divergence
    memory_one = RELAXATION[0] * stresses[1] + (1.0 - RELAXATION[0]) * MEMORY_WEIGHT[0] * material[2] * loading
    memory_two = RELAXATION[1] * stresses[2] + (1.0 - RELAXATION[1]) * MEMORY_WEIGHT[1] * material[2] * loading
    pressure = stresses[0] - TIME_STEP * (loading - memory_one - memory_two)
    return jnp.stack([pressure, memory_one, memory_two])


def pad_cells(field):
    widths = [(0, 0)] * (field.ndim - 2) + [(RADIUS, RADIUS), (RADIUS, RADIUS)]
    return jnp.pad(field, widths)


def step_section(current, material, elastic):
    if elastic:
        velocity = velocity_elastic(current[0:2], pad_cells(current[2:5]), material[0], RADIUS, NX, NZ)
        stresses = stress_elastic(current[2:5], pad_cells(velocity), material, RADIUS, NX, NZ)
    else:
        velocity = velocity_acoustic(current[0:2], pad_cells(current[2:5]), material[0], RADIUS, NX, NZ)
        stresses = stress_acoustic(current[2:5], pad_cells(velocity), material, RADIUS, NX, NZ)
    return jnp.concatenate([velocity, stresses], axis=0)


def injection_rows(source, plane_rows):
    picked = jnp.take(source, plane_rows, axis=2)
    combined = jnp.stack([picked[0], picked[1], -0.5 * (picked[2] + picked[3])])
    return jnp.transpose(combined, (0, 2, 1))


def reference(fields, media, plane_rows, box_offset):
    source = fields[0]
    sections = [fields[index] for index in range(1, N_SEC)]
    depth_ids = jnp.arange(NZ, dtype=jnp.int32)
    for step_index in range(STEPS):
        source = step_section(source, media[0], True)
        rows = injection_rows(source, plane_rows)
        for index in range(N_SEC - 1):
            evolved_far = step_section(sections[index], media[index + 1], False)
            landing = (box_offset[index] + plane_rows // 2).astype(jnp.int32)
            chosen = (landing[:, None] == depth_ids[None, :]).astype(jnp.float32)
            injected = jnp.einsum("ckx,kz->cxz", rows, chosen, precision=lax.Precision.HIGHEST)
            sections[index] = jnp.concatenate([evolved_far[0:3] + COUPLING * injected, evolved_far[3:5]], axis=0)
    return jnp.stack([source] + sections)
```

```python
import functools

import jax
import jax.numpy as jnp
from jax import lax
from jax.experimental import pallas as pl
from jax.experimental.pallas import tpu as pltpu
from jax.sharding import PartitionSpec as P

STEPS = 5
NPD = 8
CELLS = 128
REACH = 8 * STEPS
PAD = 8
OWN = PAD + REACH
HIGH = OWN + CELLS
ROWS = HIGH + REACH + PAD
SPAN = CELLS + 2 * REACH
CHUNK = 16
TAPS = (0.8, -0.2, 4.0 / 105.0, -1.0 / 280.0)
DT = 0.2
MESH = pl.DeviceIdType.MESH


def along_lanes(first, second, lane):
    out = [None, None]
    for m, tap in enumerate(TAPS, 1):
        up = [pltpu.roll(v, CELLS - m, 1) for v in (first, second)]
        down = [pltpu.roll(v, m, 1) for v in (first, second)]
        low, high = lane >= m, lane < CELLS - m
        for t in range(2):
            term = tap * (jnp.where(high, up[t], up[1 - t]) - jnp.where(low, down[t], down[1 - t]))
            out[t] = term if out[t] is None else out[t] + term
    return out


def along_rows(grid, index, start):
    out = []
    for t in range(2):
        total = None
        for m, tap in enumerate(TAPS, 1):
            term = tap * (
                grid[index, t, pl.ds(start + m, CHUNK), :] - grid[index, t, pl.ds(start - m, CHUNK), :]
            )
            total = term if total is None else total + term
        out.append(total)
    return out


def add(a, b):
    return [x + y for x, y in zip(a, b)]


def chunks(low, high, body):
    count = -(-(high - low) // CHUNK)

    def step(i, carry):
        body(pl.multiple_of(low + i * CHUNK, 8))
        return carry

    lax.fori_loop(0, count, step, 0)


def solve(
    sizes, rows_ref, offset_ref, fields_ref, media_ref, out_ref,
    grid, nat, cross, corner, sent_rows, held_rows, chosen,
    halo_send, halo_recv, row_send, row_recv,
):
    n_sec, n_gx, n_gz = sizes
    sec, gx, gz = lax.axis_index("sec"), lax.axis_index("gx"), lax.axis_index("gz")
    is_source = sec == 0
    has_left, has_right = gx > 0, gx < n_gx - 1
    odd = lax.rem(gz, 2) == 1
    sibling = jnp.where(odd, gz - 1, gz + 1)
    crossing = jnp.logical_or(gz == 1, gz == 2)
    partner = 3 - gz

    grid[...] = jnp.zeros_like(grid)
    nat[...] = jnp.zeros_like(nat)
    corner[...] = jnp.zeros_like(corner)

    barrier = pltpu.get_barrier_semaphore()

    def greet(s, x, z):
        pl.semaphore_signal(barrier, inc=1, device_id=(s, x, z), device_id_type=MESH)

    pl.when(has_left)(lambda: greet(sec, gx - 1, gz))
    pl.when(has_right)(lambda: greet(sec, gx + 1, gz))
    greet(sec, gx, sibling)
    pl.when(crossing)(lambda: greet(sec, gx, partner))

    @pl.when(is_source)
    def _():
        for s in range(1, n_sec):
            greet(s, gx, gz)

    pl.when(jnp.logical_not(is_source))(lambda: greet(0, gx, gz))

    for f in range(5):
        grid[f, 0, OWN:HIGH, :] = fields_ref[f].T
    for f in range(3):
        grid[5 + f, 0, OWN:HIGH, :] = media_ref[f].T

    lane1 = lax.broadcasted_iota(jnp.int32, (8, CELLS), 1)
    landing = jnp.full((8, CELLS), -1, jnp.int32)
    offset = offset_ref[jnp.maximum(sec - 1, 0)]
    for k in range(4 * NPD):
        spot = offset + lax.div(rows_ref[k], 2)
        mine = jnp.logical_and(lax.rem(lane1, 4 * NPD) == k, lane1 < 12 * NPD)
        landing = jnp.where(mine, spot, landing)
    depth = lax.broadcasted_iota(jnp.int32, (SPAN, CELLS), 0) + (gz * CELLS - REACH)
    hit = depth == jnp.broadcast_to(landing[0:1], (SPAN, CELLS))
    chosen[...] = jnp.where(hit, 0.5, 0.0).astype(jnp.bfloat16)

    waits = (
        1
        + has_left.astype(jnp.int32)
        + has_right.astype(jnp.int32)
        + crossing.astype(jnp.int32)
        + jnp.where(is_source, n_sec - 1, 1)
    )
    pl.semaphore_wait(barrier, waits)

    def remote(src, dst, i, where):
        return pltpu.make_async_remote_copy(
            src, dst, halo_send.at[i], halo_recv.at[i], device_id=where, device_id_type=MESH
        )

    left, right = (sec, gx - 1, gz), (sec, gx + 1, gz)
    over = (sec, gx, partner)
    near = (sec, gx, sibling)
    cross_from = pl.multiple_of(jnp.where(gz == 1, HIGH - REACH, OWN), 8)
    cross_to = pl.multiple_of(jnp.where(gz == 1, HIGH, PAD), 8)
    near_from = pl.multiple_of(jnp.where(odd, OWN, HIGH - REACH), 8)
    near_to = pl.multiple_of(jnp.where(odd, HIGH, PAD), 8)

    over_copy = remote(grid.at[:, 0, pl.ds(cross_from, REACH), :], cross, 0, over)
    pl.when(crossing)(over_copy.start)

    edge = CELLS - REACH
    left_copies = [
        remote(fields_ref.at[:, 0:REACH, :], nat.at[0:5, 0:REACH, :], 1, left),
        remote(media_ref.at[:, 0:REACH, :], nat.at[5:8, 0:REACH, :], 2, left),
    ]
    right_copies = [
        remote(fields_ref.at[:, edge:CELLS, :], nat.at[0:5, edge:CELLS, :], 3, right),
        remote(media_ref.at[:, edge:CELLS, :], nat.at[5:8, edge:CELLS, :], 4, right),
    ]

    def each(copies, name):
        def run():
            for c in copies:
                getattr(c, name)()

        return run

    pl.when(has_left)(each(left_copies, "start"))
    pl.when(has_right)(each(right_copies, "start"))
    pl.when(has_right)(each(left_copies, "wait_recv"))
    pl.when(has_left)(each(right_copies, "wait_recv"))
    for f in range(8):
        grid[f, 1, OWN:HIGH, :] = nat[f].T

    near_copy = remote(
        grid.at[:, :, pl.ds(near_from, REACH), :], grid.at[:, :, pl.ds(near_to, REACH), :], 5, near
    )
    near_copy.start()

    corner_left = remote(cross, corner.at[0], 6, left)
    corner_right = remote(cross, corner.at[1], 7, right)

    @pl.when(crossing)
    def _():
        over_copy.wait_recv()
        pl.when(has_left)(corner_left.start)
        pl.when(has_right)(corner_right.start)
        lanes = lax.broadcasted_iota(jnp.int32, (REACH, CELLS), 1)
        for f in range(8):
            grid[f, 0, pl.ds(cross_to, REACH), :] = cross[f]
        pl.when(has_right)(corner_left.wait_recv)
        pl.when(has_left)(corner_right.wait_recv)
        for f in range(8):
            joined = jnp.where(lanes < REACH, corner[0, f], jnp.where(lanes >= edge, corner[1, f], 0.0))
            grid[f, 1, pl.ds(cross_to, REACH), :] = joined

    near_copy.wait()
    pl.when(crossing)(over_copy.wait_send)

    lane = lax.broadcasted_iota(jnp.int32, (CHUNK, CELLS), 1)

    def get(f, start):
        return [grid[f, t, pl.ds(start, CHUNK), :] for t in range(2)]

    def put(f, start, values):
        for t in range(2):
            grid[f, t, pl.ds(start, CHUNK), :] = values[t]

    def row_copy(i, step, where):
        return pltpu.make_async_remote_copy(
            sent_rows.at[step], held_rows.at[step, gz], row_send.at[i, step], row_recv.at[0, step],
            device_id=where, device_id_type=MESH,
        )

    @pl.when(is_source)
    def _():
        for step in range(STEPS):
            reach = 8 * (STEPS - step)

            def velocities(start):
                buoyancy = get(5, start)
                shear = get(4, start)
                force_x = add(along_lanes(*get(2, start), lane), along_rows(grid, 4, start))
                force_z = add(along_lanes(*shear, lane), along_rows(grid, 3, start))
                put(0, start, [v + DT * b * g for v, b, g in zip(get(0, start), buoyancy, force_x)])
                put(1, start, [v + DT * b * g for v, b, g in zip(get(1, start), buoyancy, force_z)])

            def stresses(start):
                first, second = get(6, start), get(7, start)
                vx, vz = get(0, start), get(1, start)
                strain_x, strain_z = along_lanes(*vx, lane), along_rows(grid, 1, start)
                bend = add(along_rows(grid, 0, start), along_lanes(*vz, lane))
                xx, zz, xz = get(2, start), get(3, start), get(4, start)
                for t in range(2):
                    stiff = first[t] + 2.0 * second[t]
                    xx[t] = xx[t] + DT * (stiff * strain_x[t] + first[t] * strain_z[t])
                    zz[t] = zz[t] + DT * (first[t] * strain_x[t] + stiff * strain_z[t])
                    xz[t] = xz[t] + DT * second[t] * bend[t]
                put(2, start, xx)
                put(3, start, zz)
                put(4, start, xz)

            chunks(OWN - reach, HIGH + reach, velocities)
            chunks(OWN - reach + 8, HIGH + reach - 8, stresses)
            for k in range(NPD):
                row = lax.rem(rows_ref[gz * NPD + k], CELLS) + OWN
                for t in range(2):
                    line = [grid[f, t, pl.ds(row, 1), :] for f in range(4)]
                    sent_rows[step, 0, t, k : k + 1, :] = line[0]
                    sent_rows[step, 1, t, k : k + 1, :] = line[1]
                    sent_rows[step, 2, t, k : k + 1, :] = -0.5 * (line[2] + line[3])
            for s in range(1, n_sec):
                row_copy(s - 1, step, (s, gx, gz)).start()
        for step in range(STEPS):
            for s in range(1, n_sec):
                row_copy(s - 1, step, (s, gx, gz)).wait_send()

    @pl.when(jnp.logical_not(is_source))
    def _():
        half = lax.div(gz, 2) * 2
        other = 2 - half

        def hand_on(i, step, blocks, where):
            return pltpu.make_async_remote_copy(
                held_rows.at[step, blocks], held_rows.at[step, blocks], row_send.at[i - 1, step],
                row_recv.at[i, step], device_id=where, device_id_type=MESH,
            )

        def to_sibling(step):
            return hand_on(1, step, pl.ds(gz, 1), near)

        def from_sibling(step):
            return hand_on(1, step, pl.ds(sibling, 1), near)

        def to_partner(step):
            return hand_on(2, step, pl.ds(half, 2), over)

        def from_partner(step):
            return hand_on(2, step, pl.ds(other, 2), over)

        def to_rest(step):
            return hand_on(3, step, pl.ds(other, 2), near)

        def velocities(start):
            buoyancy = get(5, start)
            slope_x = along_lanes(*get(2, start), lane)
            slope_z = along_rows(grid, 2, start)
            put(0, start, [v - DT * b * g for v, b, g in zip(get(0, start), buoyancy, slope_x)])
            put(1, start, [v - DT * b * g for v, b, g in zip(get(1, start), buoyancy, slope_z)])

        def pressures(start):
            kappa, strength = get(6, start), get(7, start)
            spread = add(along_lanes(*get(0, start), lane), along_rows(grid, 1, start))
            p, one, two = get(2, start), get(3, start), get(4, start)
            for t in range(2):
                load = kappa[t] * spread[t]
                driven = strength[t] * load
                one[t] = 0.9 * one[t] + (1.0 - 0.9) * 0.15 * driven
                two[t] = 0.5 * two[t] + (1.0 - 0.5) * 0.1 * driven
                p[t] = p[t] - DT * (load - one[t] - two[t])
            put(2, start, p)
            put(3, start, one)
            put(4, start, two)

        def evolve(step):
            reach = 8 * (STEPS - step)
            chunks(OWN - reach, HIGH + reach, velocities)
            chunks(OWN - reach + 8, HIGH + reach - 8, pressures)

        evolve(0)
        for step in range(STEPS):
            row_copy(0, step, near).wait_recv()
            to_sibling(step).start()

            @pl.when(crossing)
            def _():
                from_sibling(step).wait_recv()
                to_partner(step).start()

        for step in range(STEPS):
            pl.when(jnp.logical_not(crossing))(from_sibling(step).wait_recv)

            @pl.when(crossing)
            def _():
                from_partner(step).wait_recv()
                to_rest(step).start()

            pl.when(jnp.logical_not(crossing))(to_rest(step).wait_recv)
            low = OWN - 8 * (STEPS - 1 - step)
            high = HIGH + 8 * (STEPS - 1 - step)
            pick = chosen[low - PAD : high - PAD, :]
            for c in range(3):
                for t in range(2 if step < STEPS - 1 else 1):
                    lines = held_rows[step, :, c, t].reshape(4 * NPD, CELLS)
                    top = lines.astype(jnp.bfloat16)
                    rest = lines - top.astype(jnp.float32)
                    mid = rest.astype(jnp.bfloat16)
                    last = (rest - mid.astype(jnp.float32)).astype(jnp.bfloat16)
                    stack = jnp.concatenate([top, mid, last, jnp.zeros_like(top)], axis=0)
                    grid[c, t, low:high, :] += jnp.dot(pick, stack, preferred_element_type=jnp.float32)
            if step < STEPS - 1:
                evolve(step + 1)

        for step in range(STEPS):
            to_sibling(step).wait_send()

            @pl.when(crossing)
            def _():
                to_partner(step).wait_send()
                to_rest(step).wait_send()

    for f in range(5):
        out_ref[f] = grid[f, 0, OWN:HIGH, :].T

    pl.when(has_left)(each(left_copies, "wait_send"))
    pl.when(has_right)(each(right_copies, "wait_send"))

    @pl.when(crossing)
    def _():
        pl.when(has_left)(corner_left.wait_send)
        pl.when(has_right)(corner_right.wait_send)


def solution(mesh):
    sizes = tuple(mesh.shape[a] for a in ("sec", "gx", "gz"))

    def local(fields, media, plane_rows, box_offset):
        vmem = pl.BlockSpec(memory_space=pltpu.VMEM)
        smem = pl.BlockSpec(memory_space=pltpu.SMEM)
        out = pl.pallas_call(
            functools.partial(solve, sizes),
            out_shape=jax.ShapeDtypeStruct((5, CELLS, CELLS), jnp.float32),
            in_specs=[smem, smem, vmem, vmem],
            out_specs=vmem,
            scratch_shapes=[
                pltpu.VMEM((8, 2, ROWS, CELLS), jnp.float32),
                pltpu.VMEM((8, CELLS, CELLS), jnp.float32),
                pltpu.VMEM((8, REACH, CELLS), jnp.float32),
                pltpu.VMEM((2, 8, REACH, CELLS), jnp.float32),
                pltpu.VMEM((STEPS, 3, 2, NPD, CELLS), jnp.float32),
                pltpu.VMEM((STEPS, 4, 3, 2, NPD, CELLS), jnp.float32),
                pltpu.VMEM((SPAN, CELLS), jnp.bfloat16),
                pltpu.SemaphoreType.DMA((8,)),
                pltpu.SemaphoreType.DMA((8,)),
                pltpu.SemaphoreType.DMA((3, STEPS)),
                pltpu.SemaphoreType.DMA((4, STEPS)),
            ],
            compiler_params=pltpu.CompilerParams(collective_id=0, has_side_effects=True),
        )(plane_rows, box_offset, fields[0], media[0])
        return out[None]

    spec = P("sec", None, "gx", "gz")
    return jax.shard_map(
        local, mesh=mesh, in_specs=(spec, spec, P(), P()), out_specs=spec, check_vma=False
    )
```

```python
import functools

import jax
import jax.numpy as jnp
from jax import lax
from jax.experimental import pallas as pl
from jax.experimental.pallas import tpu as pltpu
from jax.sharding import PartitionSpec as P

STEPS = 5
NPD = 8
CELLS = 128
REACH = 8 * STEPS
PAD = 8
OWN = PAD + REACH
HIGH = OWN + CELLS
ROWS = HIGH + REACH + PAD
SPAN = CELLS + 2 * REACH
CHUNK = 16
TAPS = (0.8, -0.2, 4.0 / 105.0, -1.0 / 280.0)
DT = 0.2
MESH = pl.DeviceIdType.MESH


def along_lanes(first, second, lane):
    out = [None, None]
    for m, tap in enumerate(TAPS, 1):
        up = [pltpu.roll(v, CELLS - m, 1) for v in (first, second)]
        down = [pltpu.roll(v, m, 1) for v in (first, second)]
        low, high = lane >= m, lane < CELLS - m
        for t in range(2):
            term = tap * (jnp.where(high, up[t], up[1 - t]) - jnp.where(low, down[t], down[1 - t]))
            out[t] = term if out[t] is None else out[t] + term
    return out


def along_rows(grid, index, start):
    out = []
    for t in range(2):
        total = None
        for m, tap in enumerate(TAPS, 1):
            term = tap * (
                grid[index, t, pl.ds(start + m, CHUNK), :] - grid[index, t, pl.ds(start - m, CHUNK), :]
            )
            total = term if total is None else total + term
        out.append(total)
    return out


def add(a, b):
    return [x + y for x, y in zip(a, b)]


def chunks(low, high, body, save):
    count = (high - low) // CHUNK

    def step(i, carry):
        starts = [pl.multiple_of(low + (2 * i + j) * CHUNK, 8) for j in range(2)]
        results = [body(start) for start in starts]
        for start, result in zip(starts, results):
            save(start, result)
        return carry

    lax.fori_loop(0, count // 2, step, 0)
    if count % 2:
        start = low + (count - 1) * CHUNK
        save(start, body(start))


def solve(
    sizes, rows_ref, offset_ref, fields_ref, media_ref, out_ref,
    grid, nat, cross, corner, sent_rows, held_rows, chosen,
    halo_send, halo_recv, row_send, row_recv,
):
    n_sec, n_gx, n_gz = sizes
    sec, gx, gz = lax.axis_index("sec"), lax.axis_index("gx"), lax.axis_index("gz")
    is_source = sec == 0
    has_left, has_right = gx > 0, gx < n_gx - 1
    odd = lax.rem(gz, 2) == 1
    sibling = jnp.where(odd, gz - 1, gz + 1)
    crossing = jnp.logical_or(gz == 1, gz == 2)
    partner = 3 - gz

    grid[...] = jnp.zeros_like(grid)
    nat[...] = jnp.zeros_like(nat)
    corner[...] = jnp.zeros_like(corner)

    barrier = pltpu.get_barrier_semaphore()

    def greet(s, x, z):
        pl.semaphore_signal(barrier, inc=1, device_id=(s, x, z), device_id_type=MESH)

    pl.when(has_left)(lambda: greet(sec, gx - 1, gz))
    pl.when(has_right)(lambda: greet(sec, gx + 1, gz))
    greet(sec, gx, sibling)
    pl.when(crossing)(lambda: greet(sec, gx, partner))

    @pl.when(is_source)
    def _():
        for s in range(1, n_sec):
            greet(s, gx, gz)

    @pl.when(jnp.logical_not(is_source))
    def _():
        greet(0, gx, gz)
        for o in range(1, n_sec - 1):
            s = 1 + lax.rem(sec - 1 + o, n_sec - 1)
            greet(s, gx, gz)
            greet(s, gx, sibling)


    for f in range(5):
        grid[f, 0, OWN:HIGH, :] = fields_ref[f].T
    for f in range(3):
        grid[5 + f, 0, OWN:HIGH, :] = media_ref[f].T

    lane1 = lax.broadcasted_iota(jnp.int32, (8, CELLS), 1)
    landing = jnp.full((8, CELLS), -1, jnp.int32)
    offset = offset_ref[jnp.maximum(sec - 1, 0)]
    for k in range(4 * NPD):
        spot = offset + lax.div(rows_ref[k], 2)
        mine = jnp.logical_and(lax.rem(lane1, 4 * NPD) == k, lane1 < 12 * NPD)
        landing = jnp.where(mine, spot, landing)
    depth = lax.broadcasted_iota(jnp.int32, (SPAN, CELLS), 0) + (gz * CELLS - REACH)
    hit = depth == jnp.broadcast_to(landing[0:1], (SPAN, CELLS))
    chosen[...] = jnp.where(hit, 0.5, 0.0).astype(jnp.bfloat16)

    waits = (
        1
        + has_left.astype(jnp.int32)
        + has_right.astype(jnp.int32)
        + crossing.astype(jnp.int32)
        + jnp.where(is_source, n_sec - 1, 1 + 2 * (n_sec - 2))
    )
    pl.semaphore_wait(barrier, waits)

    def remote(src, dst, i, where):
        return pltpu.make_async_remote_copy(
            src, dst, halo_send.at[i], halo_recv.at[i], device_id=where, device_id_type=MESH
        )

    left, right = (sec, gx - 1, gz), (sec, gx + 1, gz)
    over = (sec, gx, partner)
    near = (sec, gx, sibling)
    cross_from = pl.multiple_of(jnp.where(gz == 1, HIGH - REACH, OWN), 8)
    cross_to = pl.multiple_of(jnp.where(gz == 1, HIGH, PAD), 8)
    near_from = pl.multiple_of(jnp.where(odd, OWN, HIGH - REACH), 8)
    near_to = pl.multiple_of(jnp.where(odd, HIGH, PAD), 8)

    over_copy = remote(grid.at[:, 0, pl.ds(cross_from, REACH), :], cross, 0, over)
    pl.when(crossing)(over_copy.start)

    edge = CELLS - REACH
    left_copies = [
        remote(fields_ref.at[:, 0:REACH, :], nat.at[0:5, 0:REACH, :], 1, left),
        remote(media_ref.at[:, 0:REACH, :], nat.at[5:8, 0:REACH, :], 2, left),
    ]
    right_copies = [
        remote(fields_ref.at[:, edge:CELLS, :], nat.at[0:5, edge:CELLS, :], 3, right),
        remote(media_ref.at[:, edge:CELLS, :], nat.at[5:8, edge:CELLS, :], 4, right),
    ]

    def each(copies, name):
        def run():
            for c in copies:
                getattr(c, name)()

        return run

    pl.when(has_left)(each(left_copies, "start"))
    pl.when(has_right)(each(right_copies, "start"))
    pl.when(has_right)(each(left_copies, "wait_recv"))
    pl.when(has_left)(each(right_copies, "wait_recv"))
    for f in range(8):
        grid[f, 1, OWN:HIGH, :] = nat[f].T

    near_copy = remote(
        grid.at[:, :, pl.ds(near_from, REACH), :], grid.at[:, :, pl.ds(near_to, REACH), :], 5, near
    )
    near_copy.start()

    corner_left = remote(cross, corner.at[0], 6, left)
    corner_right = remote(cross, corner.at[1], 7, right)

    @pl.when(crossing)
    def _():
        over_copy.wait_recv()
        pl.when(has_left)(corner_left.start)
        pl.when(has_right)(corner_right.start)
        lanes = lax.broadcasted_iota(jnp.int32, (REACH, CELLS), 1)
        for f in range(8):
            grid[f, 0, pl.ds(cross_to, REACH), :] = cross[f]
        pl.when(has_right)(corner_left.wait_recv)
        pl.when(has_left)(corner_right.wait_recv)
        for f in range(8):
            joined = jnp.where(lanes < REACH, corner[0, f], jnp.where(lanes >= edge, corner[1, f], 0.0))
            grid[f, 1, pl.ds(cross_to, REACH), :] = joined

    near_copy.wait()
    pl.when(crossing)(over_copy.wait_send)

    lane = lax.broadcasted_iota(jnp.int32, (CHUNK, CELLS), 1)

    def get(f, start):
        return [grid[f, t, pl.ds(start, CHUNK), :] for t in range(2)]

    def save(start, fields):
        for f, values in fields.items():
            for t in range(2):
                grid[f, t, pl.ds(start, CHUNK), :] = values[t]

    def tiles(step):
        return pl.ds(0, 2 if step < STEPS - 1 else 1)

    def row_copy(i, step, where):
        return pltpu.make_async_remote_copy(
            sent_rows.at[step, tiles(step)], held_rows.at[step, tiles(step), gz], row_send.at[i, step], row_recv.at[0, step],
            device_id=where, device_id_type=MESH,
        )

    @pl.when(is_source)
    def _():
        for step in range(STEPS):
            reach = 8 * (STEPS - step)

            def velocities(start):
                buoyancy = get(5, start)
                shear = get(4, start)
                force_x = add(along_lanes(*get(2, start), lane), along_rows(grid, 4, start))
                force_z = add(along_lanes(*shear, lane), along_rows(grid, 3, start))
                return {
                    0: [v + DT * b * g for v, b, g in zip(get(0, start), buoyancy, force_x)],
                    1: [v + DT * b * g for v, b, g in zip(get(1, start), buoyancy, force_z)],
                }

            def stresses(start):
                first, second = get(6, start), get(7, start)
                vx, vz = get(0, start), get(1, start)
                strain_x, strain_z = along_lanes(*vx, lane), along_rows(grid, 1, start)
                bend = add(along_rows(grid, 0, start), along_lanes(*vz, lane))
                xx, zz, xz = get(2, start), get(3, start), get(4, start)
                for t in range(2):
                    stiff = first[t] + 2.0 * second[t]
                    xx[t] = xx[t] + DT * (stiff * strain_x[t] + first[t] * strain_z[t])
                    zz[t] = zz[t] + DT * (first[t] * strain_x[t] + stiff * strain_z[t])
                    xz[t] = xz[t] + DT * second[t] * bend[t]
                return {2: xx, 3: zz, 4: xz}

            chunks(OWN - reach, HIGH + reach, velocities, save)
            chunks(OWN - reach + 8, HIGH + reach - 8, stresses, save)
            for k in range(NPD):
                row = lax.rem(rows_ref[gz * NPD + k], CELLS) + OWN
                for t in range(2):
                    line = [grid[f, t, pl.ds(row, 1), :] for f in range(4)]
                    sent_rows[step, t, 0, k : k + 1, :] = line[0]
                    sent_rows[step, t, 1, k : k + 1, :] = line[1]
                    sent_rows[step, t, 2, k : k + 1, :] = -0.5 * (line[2] + line[3])
            for s in range(1, n_sec):
                row_copy(s - 1, step, (s, gx, gz)).start()
        for step in range(STEPS):
            for s in range(1, n_sec):
                row_copy(s - 1, step, (s, gx, gz)).wait_send()

    @pl.when(jnp.logical_not(is_source))
    def _():
        half = lax.div(gz, 2) * 2
        other = 2 - half

        part = sec - 1
        others = [lax.rem(part + 1, 3), lax.rem(part + 2, 3)]

        def hand_on(i, step, blocks, parts, where):
            piece = held_rows.at[step, tiles(step), blocks, parts]
            return pltpu.make_async_remote_copy(
                piece, piece, row_send.at[i, step], row_recv.at[i, step], device_id=where, device_id_type=MESH
            )

        whole = pl.ds(0, 3)

        def to_sibling(step):
            return hand_on(1, step, pl.ds(gz, 1), whole, near)

        def from_sibling(step):
            return hand_on(1, step, pl.ds(sibling, 1), whole, near)

        def to_partner(step):
            return hand_on(2, step, pl.ds(gz, 1), pl.ds(part, 1), over)

        def from_partner(step):
            return hand_on(2, step, pl.ds(partner, 1), pl.ds(part, 1), over)

        def nearby_to_partner(step):
            return hand_on(3, step, pl.ds(sibling, 1), pl.ds(part, 1), over)

        def nearby_from_partner(step):
            return hand_on(3, step, pl.ds(3 - sibling, 1), pl.ds(part, 1), over)

        def spread(step):
            piece = held_rows.at[step, tiles(step), pl.ds(other, 2), pl.ds(part, 1)]
            places = [near] + [(1 + o, gx, z) for o in others for z in (gz, sibling)]
            return [
                pltpu.make_async_remote_copy(
                    piece, piece, row_send.at[i, step], row_recv.at[4 + part, step],
                    device_id=place, device_id_type=MESH,
                )
                for i, place in zip((0, 4, 5, 6, 7), places)
            ]

        def spread_in(step, which):
            piece = held_rows.at[step, tiles(step), pl.ds(other, 2), pl.ds(which, 1)]
            return pltpu.make_async_remote_copy(
                piece, piece, row_send.at[0, step], row_recv.at[4 + which, step],
                device_id=near, device_id_type=MESH,
            )

        def velocities(start):
            buoyancy = get(5, start)
            slope_x = along_lanes(*get(2, start), lane)
            slope_z = along_rows(grid, 2, start)
            return {
                0: [v - DT * b * g for v, b, g in zip(get(0, start), buoyancy, slope_x)],
                1: [v - DT * b * g for v, b, g in zip(get(1, start), buoyancy, slope_z)],
            }

        def pressures(start):
            kappa, strength = get(6, start), get(7, start)
            spread = add(along_lanes(*get(0, start), lane), along_rows(grid, 1, start))
            p, one, two = get(2, start), get(3, start), get(4, start)
            for t in range(2):
                load = kappa[t] * spread[t]
                driven = strength[t] * load
                one[t] = 0.9 * one[t] + (1.0 - 0.9) * 0.15 * driven
                two[t] = 0.5 * two[t] + (1.0 - 0.5) * 0.1 * driven
                p[t] = p[t] - DT * (load - one[t] - two[t])
            return {2: p, 3: one, 4: two}

        def evolve(step):
            reach = 8 * (STEPS - step)
            chunks(OWN - reach, HIGH + reach, velocities, save)
            chunks(OWN - reach + 8, HIGH + reach - 8, pressures, save)

        evolve(0)

        @pl.when(crossing)
        def _():
            for step in range(STEPS):
                from_sibling(step).wait_recv()
                nearby_to_partner(step).start()

        for step in range(STEPS):
            row_copy(0, step, near).wait_recv()
            pl.when(crossing)(to_partner(step).start)
            to_sibling(step).start()

        def pass_on(step):
            @pl.when(crossing)
            def _():
                nearby_from_partner(step).wait_recv()
                from_partner(step).wait_recv()
                for c in spread(step):
                    c.start()

        pass_on(0)
        for step in range(STEPS):
            if step < STEPS - 1:
                pass_on(step + 1)
            pl.when(jnp.logical_not(crossing))(from_sibling(step).wait_recv)
            for which in others:
                spread_in(step, which).wait_recv()
            pl.when(jnp.logical_not(crossing))(spread_in(step, part).wait_recv)
            low = OWN - 8 * (STEPS - 1 - step)
            high = HIGH + 8 * (STEPS - 1 - step)
            pick = chosen[low - PAD : high - PAD, :]
            for c in range(3):
                for t in range(2 if step < STEPS - 1 else 1):
                    lines = held_rows[step, t, :, c].reshape(4 * NPD, CELLS)
                    top = lines.astype(jnp.bfloat16)
                    rest = lines - top.astype(jnp.float32)
                    mid = rest.astype(jnp.bfloat16)
                    last = (rest - mid.astype(jnp.float32)).astype(jnp.bfloat16)
                    stack = jnp.concatenate([top, mid, last, jnp.zeros_like(top)], axis=0)
                    grid[c, t, low:high, :] += jnp.dot(pick, stack, preferred_element_type=jnp.float32)
            if step < STEPS - 1:
                evolve(step + 1)

        for step in range(STEPS):
            to_sibling(step).wait_send()

            @pl.when(crossing)
            def _():
                to_partner(step).wait_send()
                nearby_to_partner(step).wait_send()
                for c in spread(step):
                    c.wait_send()

    for f in range(5):
        out_ref[f] = grid[f, 0, OWN:HIGH, :].T

    pl.when(has_left)(each(left_copies, "wait_send"))
    pl.when(has_right)(each(right_copies, "wait_send"))

    @pl.when(crossing)
    def _():
        pl.when(has_left)(corner_left.wait_send)
        pl.when(has_right)(corner_right.wait_send)


def solution(mesh):
    sizes = tuple(mesh.shape[a] for a in ("sec", "gx", "gz"))

    def local(fields, media, plane_rows, box_offset):
        vmem = pl.BlockSpec(memory_space=pltpu.VMEM)
        smem = pl.BlockSpec(memory_space=pltpu.SMEM)
        out = pl.pallas_call(
            functools.partial(solve, sizes),
            out_shape=jax.ShapeDtypeStruct((5, CELLS, CELLS), jnp.float32),
            in_specs=[smem, smem, vmem, vmem],
            out_specs=vmem,
            scratch_shapes=[
                pltpu.VMEM((8, 2, ROWS, CELLS), jnp.float32),
                pltpu.VMEM((8, CELLS, CELLS), jnp.float32),
                pltpu.VMEM((8, REACH, CELLS), jnp.float32),
                pltpu.VMEM((2, 8, REACH, CELLS), jnp.float32),
                pltpu.VMEM((STEPS, 2, 3, NPD, CELLS), jnp.float32),
                pltpu.VMEM((STEPS, 2, 4, 3, NPD, CELLS), jnp.float32),
                pltpu.VMEM((SPAN, CELLS), jnp.bfloat16),
                pltpu.SemaphoreType.DMA((8,)),
                pltpu.SemaphoreType.DMA((8,)),
                pltpu.SemaphoreType.DMA((8, STEPS)),
                pltpu.SemaphoreType.DMA((8, STEPS)),
            ],
            compiler_params=pltpu.CompilerParams(collective_id=0, has_side_effects=True),
        )(plane_rows, box_offset, fields[0], media[0])
        return out[None]

    spec = P("sec", None, "gx", "gz")
    return jax.shard_map(
        local, mesh=mesh, in_specs=(spec, spec, P(), P()), out_specs=spec, check_vma=False
    )
```

```python
import functools

import jax
import jax.numpy as jnp
from jax import lax
from jax.experimental import pallas as pl
from jax.experimental.pallas import tpu as pltpu
from jax.sharding import PartitionSpec as P

STEPS = 5
NPD = 8
CELLS = 128
REACH = 8 * STEPS
PAD = 8
OWN = PAD + REACH
HIGH = OWN + CELLS
ROWS = HIGH + REACH + PAD
SPAN = CELLS + 2 * REACH
CHUNK = 16
TAPS = (0.8, -0.2, 4.0 / 105.0, -1.0 / 280.0)
DT = 0.2
MESH = pl.DeviceIdType.MESH


def along_lanes(first, second, lane):
    out = [None, None]
    for m, tap in enumerate(TAPS, 1):
        up = [pltpu.roll(v, CELLS - m, 1) for v in (first, second)]
        down = [pltpu.roll(v, m, 1) for v in (first, second)]
        low, high = lane >= m, lane < CELLS - m
        for t in range(2):
            term = tap * (jnp.where(high, up[t], up[1 - t]) - jnp.where(low, down[t], down[1 - t]))
            out[t] = term if out[t] is None else out[t] + term
    return out


def along_rows(grid, index, start):
    out = []
    for t in range(2):
        total = None
        for m, tap in enumerate(TAPS, 1):
            term = tap * (
                grid[index, t, pl.ds(start + m, CHUNK), :] - grid[index, t, pl.ds(start - m, CHUNK), :]
            )
            total = term if total is None else total + term
        out.append(total)
    return out


def add(a, b):
    return [x + y for x, y in zip(a, b)]


def chunks(low, high, body, save):
    count = (high - low) // CHUNK

    def step(i, carry):
        starts = [pl.multiple_of(low + (2 * i + j) * CHUNK, 8) for j in range(2)]
        results = [body(start) for start in starts]
        for start, result in zip(starts, results):
            save(start, result)
        return carry

    lax.fori_loop(0, count // 2, step, 0)
    if count % 2:
        start = low + (count - 1) * CHUNK
        save(start, body(start))


def solve(
    sizes, rows_ref, offset_ref, fields_ref, media_ref, out_ref,
    grid, nat, cross, corner, sent_rows, held_rows, chosen,
    halo_send, halo_recv, row_send, row_recv,
):
    n_sec, n_gx, n_gz = sizes
    sec, gx, gz = lax.axis_index("sec"), lax.axis_index("gx"), lax.axis_index("gz")
    is_source = sec == 0
    has_left, has_right = gx > 0, gx < n_gx - 1
    odd = lax.rem(gz, 2) == 1
    sibling = jnp.where(odd, gz - 1, gz + 1)
    lower, upper = gz == 1, gz == 2
    crossing = jnp.logical_or(lower, upper)
    partner = 3 - gz

    barrier = pltpu.get_barrier_semaphore()

    def greet(s, x, z):
        pl.semaphore_signal(barrier, inc=1, device_id=(s, x, z), device_id_type=MESH)

    cross[...] = jnp.zeros_like(cross)
    pl.when(crossing)(lambda: greet(sec, gx, partner))
    grid[...] = jnp.zeros_like(grid)
    nat[...] = jnp.zeros_like(nat)

    @pl.when(jnp.logical_not(has_right))
    def _():
        corner[0] = jnp.zeros_like(corner[0])

    @pl.when(jnp.logical_not(has_left))
    def _():
        corner[1] = jnp.zeros_like(corner[1])

    pl.when(has_left)(lambda: greet(sec, gx - 1, gz))
    pl.when(has_right)(lambda: greet(sec, gx + 1, gz))
    greet(sec, gx, sibling)

    @pl.when(is_source)
    def _():
        for s in range(1, n_sec):
            greet(s, gx, gz)

    @pl.when(jnp.logical_not(is_source))
    def _():
        greet(0, gx, gz)
        for o in range(1, n_sec - 1):
            s = 1 + lax.rem(sec - 1 + o, n_sec - 1)
            greet(s, gx, gz)
            greet(s, gx, sibling)


    for f in range(5):
        grid[f, 0, OWN:HIGH, :] = fields_ref[f].T
    for f in range(3):
        grid[5 + f, 0, OWN:HIGH, :] = media_ref[f].T

    lane1 = lax.broadcasted_iota(jnp.int32, (8, CELLS), 1)
    landing = jnp.full((8, CELLS), -1, jnp.int32)
    offset = offset_ref[jnp.maximum(sec - 1, 0)]
    for k in range(4 * NPD):
        spot = offset + lax.div(rows_ref[k], 2)
        mine = jnp.logical_and(lax.rem(lane1, 4 * NPD) == k, lane1 < 12 * NPD)
        landing = jnp.where(mine, spot, landing)
    depth = lax.broadcasted_iota(jnp.int32, (SPAN, CELLS), 0) + (gz * CELLS - REACH)
    hit = depth == jnp.broadcast_to(landing[0:1], (SPAN, CELLS))
    chosen[...] = jnp.where(hit, 0.5, 0.0).astype(jnp.bfloat16)

    waits = (
        1
        + has_left.astype(jnp.int32)
        + has_right.astype(jnp.int32)
        + crossing.astype(jnp.int32)
        + jnp.where(is_source, n_sec - 1, 1 + 2 * (n_sec - 2))
    )
    pl.semaphore_wait(barrier, waits)

    def remote(src, dst, i, where):
        return pltpu.make_async_remote_copy(
            src, dst, halo_send.at[i], halo_recv.at[i], device_id=where, device_id_type=MESH
        )

    left, right = (sec, gx - 1, gz), (sec, gx + 1, gz)
    over = (sec, gx, partner)
    near = (sec, gx, sibling)
    cross_to = pl.multiple_of(jnp.where(gz == 1, HIGH, PAD), 8)
    near_from = pl.multiple_of(jnp.where(odd, OWN, HIGH - REACH), 8)
    near_to = pl.multiple_of(jnp.where(odd, HIGH, PAD), 8)

    edge = CELLS - REACH
    left_copies = [
        remote(fields_ref.at[:, 0:REACH, :], nat.at[0:5, 0:REACH, :], 24, left),
        remote(media_ref.at[:, 0:REACH, :], nat.at[5:8, 0:REACH, :], 25, left),
    ]
    right_copies = [
        remote(fields_ref.at[:, edge:CELLS, :], nat.at[0:5, edge:CELLS, :], 26, right),
        remote(media_ref.at[:, edge:CELLS, :], nat.at[5:8, edge:CELLS, :], 27, right),
    ]

    def each(copies, name):
        def run():
            for c in copies:
                getattr(c, name)()

        return run

    deep = {0: 40, 1: 40, 2: 40, 3: 40, 4: 40, 5: 40, 6: 32, 7: 32}
    flat = {0: 32, 1: 40, 2: 40, 3: 32, 4: 32, 5: 40, 6: 32, 7: 32}

    def depths(f, act):
        if deep[f] == flat[f]:
            act(deep[f])
        else:
            pl.when(is_source)(lambda: act(deep[f]))
            pl.when(jnp.logical_not(is_source))(lambda: act(flat[f]))

    def over_copy(f, depth, low):
        if low:
            src, dst = grid.at[f, 0, HIGH - depth : HIGH, :], cross.at[f, REACH - depth : REACH, :]
        else:
            src, dst = grid.at[f, 0, OWN : OWN + depth, :], cross.at[f, 0:depth, :]
        return remote(src, dst, f, over)

    def corner_copy(f, depth, low, side):
        rows = pl.ds(0, depth) if low else pl.ds(REACH - depth, depth)
        place = left if side == 0 else right
        return remote(cross.at[f, rows, :], corner.at[side, f, rows, :], 8 + 8 * side + f, place)

    def over_start(low):
        for f in range(8):
            depths(f, lambda depth: over_copy(f, depth, low).start())

    pl.when(upper)(lambda: over_start(False))
    pl.when(lower)(lambda: over_start(True))
    pl.when(has_left)(each(left_copies, "start"))
    pl.when(has_right)(each(right_copies, "start"))


    pl.when(has_right)(each(left_copies, "wait_recv"))
    pl.when(has_left)(each(right_copies, "wait_recv"))
    for f in range(8):
        grid[f, 1, OWN:HIGH, :] = nat[f].T

    near_copy = remote(
        grid.at[:, :, pl.ds(near_from, REACH), :], grid.at[:, :, pl.ds(near_to, REACH), :], 28, near
    )
    near_copy.start()

    lanes = lax.broadcasted_iota(jnp.int32, (REACH, CELLS), 1)

    def take_halo(low):
        for f in range(8):

            def arrive(depth):
                over_copy(f, depth, not low).wait_recv()
                pl.when(has_left)(corner_copy(f, depth, low, 0).start)
                pl.when(has_right)(corner_copy(f, depth, low, 1).start)

            depths(f, arrive)
            grid[f, 0, pl.ds(cross_to, REACH), :] = cross[f]
        for f in range(8):

            def arrive(depth):
                pl.when(has_right)(corner_copy(f, depth, low, 0).wait_recv)
                pl.when(has_left)(corner_copy(f, depth, low, 1).wait_recv)

            depths(f, arrive)
            joined = jnp.where(lanes < REACH, corner[0, f], jnp.where(lanes >= edge, corner[1, f], 0.0))
            grid[f, 1, pl.ds(cross_to, REACH), :] = joined

        for f in range(8):

            def leave(depth):
                over_copy(f, depth, low).wait_send()
                pl.when(has_left)(corner_copy(f, depth, low, 0).wait_send)
                pl.when(has_right)(corner_copy(f, depth, low, 1).wait_send)

            depths(f, leave)

    pl.when(lower)(lambda: take_halo(True))
    pl.when(upper)(lambda: take_halo(False))
    near_copy.wait()

    lane = lax.broadcasted_iota(jnp.int32, (CHUNK, CELLS), 1)

    def get(f, start):
        return [grid[f, t, pl.ds(start, CHUNK), :] for t in range(2)]

    def save(start, fields):
        for f, values in fields.items():
            for t, value in enumerate(values):
                grid[f, t, pl.ds(start, CHUNK), :] = value

    def tiles(step):
        return pl.ds(0, 2 if step < STEPS - 1 else 1)

    def row_copy(i, step, where):
        return pltpu.make_async_remote_copy(
            sent_rows.at[step, tiles(step)], held_rows.at[step, tiles(step), gz], row_send.at[i, step], row_recv.at[0, step],
            device_id=where, device_id_type=MESH,
        )

    def crossed(step, part):
        return pl.ds(part, 1) if step < STEPS - 1 else pl.ds(0, 3)

    def row_over(step, s):
        parts = crossed(step, s - 1)
        return pltpu.make_async_remote_copy(
            sent_rows.at[step, tiles(step), parts], held_rows.at[step, tiles(step), gz, parts],
            row_send.at[2 + s, step], row_recv.at[2, step],
            device_id=(s, gx, partner), device_id_type=MESH,
        )

    @pl.when(is_source)
    def _():
        for step in range(STEPS):
            reach = 8 * (STEPS - step)

            def velocities(start):
                buoyancy = get(5, start)
                shear = get(4, start)
                force_x = add(along_lanes(*get(2, start), lane), along_rows(grid, 4, start))
                force_z = add(along_lanes(*shear, lane), along_rows(grid, 3, start))
                return {
                    0: [v + DT * b * g for v, b, g in zip(get(0, start), buoyancy, force_x)],
                    1: [v + DT * b * g for v, b, g in zip(get(1, start), buoyancy, force_z)],
                }

            def stresses(start):
                count = 2 if step < STEPS - 1 else 1
                first, second = get(6, start), get(7, start)
                vx, vz = get(0, start), get(1, start)
                strain_x, strain_z = along_lanes(*vx, lane), along_rows(grid, 1, start)
                bend = add(along_rows(grid, 0, start), along_lanes(*vz, lane))
                xx, zz, xz = (get(f, start)[:count] for f in (2, 3, 4))
                for t in range(count):
                    stiff = first[t] + 2.0 * second[t]
                    xx[t] = xx[t] + DT * (stiff * strain_x[t] + first[t] * strain_z[t])
                    zz[t] = zz[t] + DT * (first[t] * strain_x[t] + stiff * strain_z[t])
                    xz[t] = xz[t] + DT * second[t] * bend[t]
                return {2: xx, 3: zz, 4: xz}

            chunks(OWN - reach, HIGH + reach, velocities, save)
            chunks(OWN - reach + 8, HIGH + reach - 8, stresses, save)
            for k in range(NPD):
                row = lax.rem(rows_ref[gz * NPD + k], CELLS) + OWN
                for t in range(2):
                    line = [grid[f, t, pl.ds(row, 1), :] for f in range(4)]
                    sent_rows[step, t, 0, k : k + 1, :] = line[0]
                    sent_rows[step, t, 1, k : k + 1, :] = line[1]
                    sent_rows[step, t, 2, k : k + 1, :] = -0.5 * (line[2] + line[3])

            @pl.when(crossing)
            def _():
                for s in range(1, n_sec):
                    row_over(step, s).start()

            for s in range(1, n_sec):
                row_copy(s - 1, step, (s, gx, gz)).start()
        for step in range(STEPS):
            for s in range(1, n_sec):
                row_copy(s - 1, step, (s, gx, gz)).wait_send()
                pl.when(crossing)(row_over(step, s).wait_send)

    @pl.when(jnp.logical_not(is_source))
    def _():
        half = lax.div(gz, 2) * 2
        other = 2 - half

        part = sec - 1
        others = [lax.rem(part + 1, 3), lax.rem(part + 2, 3)]

        def hand_on(i, step, blocks, parts, where):
            piece = held_rows.at[step, tiles(step), blocks, parts]
            return pltpu.make_async_remote_copy(
                piece, piece, row_send.at[i, step], row_recv.at[i, step], device_id=where, device_id_type=MESH
            )

        whole = pl.ds(0, 3)

        def to_sibling(step):
            return hand_on(1, step, pl.ds(gz, 1), whole, near)

        def from_sibling(step):
            return hand_on(1, step, pl.ds(sibling, 1), whole, near)

        def from_partner(step):
            return hand_on(2, step, pl.ds(partner, 1), crossed(step, part), over)

        def nearby_to_partner(step):
            return hand_on(3, step, pl.ds(sibling, 1), crossed(step, part), over)

        def nearby_from_partner(step):
            return hand_on(3, step, pl.ds(3 - sibling, 1), crossed(step, part), over)

        def spread(step):
            piece = held_rows.at[step, tiles(step), pl.ds(other, 2), crossed(step, part)]
            places = [near]
            if step < STEPS - 1:
                places += [(1 + o, gx, z) for o in others for z in (gz, sibling)]
            return [
                pltpu.make_async_remote_copy(
                    piece, piece, row_send.at[i, step], row_recv.at[4 + part, step],
                    device_id=place, device_id_type=MESH,
                )
                for i, place in zip((0, 4, 5, 6, 7), places)
            ]

        def spread_in(step, which):
            parts = pl.ds(which, 1) if step < STEPS - 1 else whole
            piece = held_rows.at[step, tiles(step), pl.ds(other, 2), parts]
            return pltpu.make_async_remote_copy(
                piece, piece, row_send.at[0, step], row_recv.at[4 + which, step],
                device_id=near, device_id_type=MESH,
            )

        def velocities(start):
            buoyancy = get(5, start)
            slope_x = along_lanes(*get(2, start), lane)
            slope_z = along_rows(grid, 2, start)
            return {
                0: [v - DT * b * g for v, b, g in zip(get(0, start), buoyancy, slope_x)],
                1: [v - DT * b * g for v, b, g in zip(get(1, start), buoyancy, slope_z)],
            }

        def pressures(count, start):
            kappa, strength = get(6, start), get(7, start)
            spread = add(along_lanes(*get(0, start), lane), along_rows(grid, 1, start))
            p, one, two = (get(f, start)[:count] for f in (2, 3, 4))
            for t in range(count):
                load = kappa[t] * spread[t]
                driven = strength[t] * load
                one[t] = 0.9 * one[t] + (1.0 - 0.9) * 0.15 * driven
                two[t] = 0.5 * two[t] + (1.0 - 0.5) * 0.1 * driven
                p[t] = p[t] - DT * (load - one[t] - two[t])
            return {2: p, 3: one, 4: two}

        def evolve(step):
            reach = 8 * (STEPS - step)
            chunks(OWN - reach, HIGH + reach, velocities, save)
            count = 2 if step < STEPS - 1 else 1
            chunks(OWN - reach + 8, HIGH + reach - 8, functools.partial(pressures, count), save)

        evolve(0)

        @pl.when(crossing)
        def _():
            for step in range(STEPS):
                from_sibling(step).wait_recv()
                nearby_to_partner(step).start()

        for step in range(STEPS):
            row_copy(0, step, near).wait_recv()
            to_sibling(step).start()

        def pass_on(step):
            @pl.when(crossing)
            def _():
                nearby_from_partner(step).wait_recv()
                from_partner(step).wait_recv()
                for c in spread(step):
                    c.start()

        pass_on(0)
        for step in range(STEPS):
            if step < STEPS - 1:
                pass_on(step + 1)
            pl.when(jnp.logical_not(crossing))(from_sibling(step).wait_recv)
            for which in others if step < STEPS - 1 else []:
                spread_in(step, which).wait_recv()
            pl.when(jnp.logical_not(crossing))(spread_in(step, part).wait_recv)
            low = OWN - 8 * (STEPS - 1 - step)
            high = HIGH + 8 * (STEPS - 1 - step)
            pick = chosen[low - PAD : high - PAD, :]
            for c in range(3):
                for t in range(2 if step < STEPS - 1 else 1):
                    lines = held_rows[step, t, :, c].reshape(4 * NPD, CELLS)
                    top = lines.astype(jnp.bfloat16)
                    rest = lines - top.astype(jnp.float32)
                    mid = rest.astype(jnp.bfloat16)
                    last = (rest - mid.astype(jnp.float32)).astype(jnp.bfloat16)
                    stack = jnp.concatenate([top, mid, last, jnp.zeros_like(top)], axis=0)
                    grid[c, t, low:high, :] += jnp.dot(pick, stack, preferred_element_type=jnp.float32)
            if step < STEPS - 1:
                evolve(step + 1)

        for step in range(STEPS):
            to_sibling(step).wait_send()

            @pl.when(crossing)
            def _():
                nearby_to_partner(step).wait_send()
                for c in spread(step):
                    c.wait_send()

    for f in range(5):
        out_ref[f] = grid[f, 0, OWN:HIGH, :].T

    pl.when(has_left)(each(left_copies, "wait_send"))
    pl.when(has_right)(each(right_copies, "wait_send"))


def solution(mesh):
    sizes = tuple(mesh.shape[a] for a in ("sec", "gx", "gz"))

    def local(fields, media, plane_rows, box_offset):
        vmem = pl.BlockSpec(memory_space=pltpu.VMEM)
        smem = pl.BlockSpec(memory_space=pltpu.SMEM)
        out = pl.pallas_call(
            functools.partial(solve, sizes),
            out_shape=jax.ShapeDtypeStruct((5, CELLS, CELLS), jnp.float32),
            in_specs=[smem, smem, vmem, vmem],
            out_specs=vmem,
            scratch_shapes=[
                pltpu.VMEM((8, 2, ROWS, CELLS), jnp.float32),
                pltpu.VMEM((8, CELLS, CELLS), jnp.float32),
                pltpu.VMEM((8, REACH, CELLS), jnp.float32),
                pltpu.VMEM((2, 8, REACH, CELLS), jnp.float32),
                pltpu.VMEM((STEPS, 2, 3, NPD, CELLS), jnp.float32),
                pltpu.VMEM((STEPS, 2, 4, 3, NPD, CELLS), jnp.float32),
                pltpu.VMEM((SPAN, CELLS), jnp.bfloat16),
                pltpu.SemaphoreType.DMA((29,)),
                pltpu.SemaphoreType.DMA((29,)),
                pltpu.SemaphoreType.DMA((8, STEPS)),
                pltpu.SemaphoreType.DMA((8, STEPS)),
            ],
            compiler_params=pltpu.CompilerParams(collective_id=0, has_side_effects=True),
        )(plane_rows, box_offset, fields[0], media[0])
        return out[None]

    spec = P("sec", None, "gx", "gz")
    return jax.shard_map(
        local, mesh=mesh, in_specs=(spec, spec, P(), P()), out_specs=spec, check_vma=False
    )
```

```python
import functools

import jax
import jax.numpy as jnp
from jax import lax
from jax.experimental import pallas as pl
from jax.experimental.pallas import tpu as pltpu
from jax.sharding import PartitionSpec as P

STEPS = 5
NPD = 8
CELLS = 128
REACH = 8 * STEPS
PAD = 8
OWN = PAD + REACH
HIGH = OWN + CELLS
ROWS = HIGH + REACH + PAD
SPAN = CELLS + 2 * REACH
CHUNK = 16
TAPS = (0.8, -0.2, 4.0 / 105.0, -1.0 / 280.0)
DT = 0.2
MESH = pl.DeviceIdType.MESH


def along_lanes(first, second, lane):
    out = [None, None]
    for m, tap in enumerate(TAPS, 1):
        up = [pltpu.roll(v, CELLS - m, 1) for v in (first, second)]
        down = [pltpu.roll(v, m, 1) for v in (first, second)]
        low, high = lane >= m, lane < CELLS - m
        for t in range(2):
            term = tap * (jnp.where(high, up[t], up[1 - t]) - jnp.where(low, down[t], down[1 - t]))
            out[t] = term if out[t] is None else out[t] + term
    return out


def along_rows(grid, index, start):
    out = []
    for t in range(2):
        total = None
        for m, tap in enumerate(TAPS, 1):
            term = tap * (
                grid[index, t, pl.ds(start + m, CHUNK), :] - grid[index, t, pl.ds(start - m, CHUNK), :]
            )
            total = term if total is None else total + term
        out.append(total)
    return out


def add(a, b):
    return [x + y for x, y in zip(a, b)]


def chunks(low, high, body, save):
    count = (high - low) // CHUNK

    def run(first, size):
        starts = [pl.multiple_of(low + (first + j) * CHUNK, 8) for j in range(size)]
        results = [body(start) for start in starts]
        for start, result in zip(starts, results):
            save(start, result)

    def step(i, carry):
        run(3 * i, 3)
        return carry

    lax.fori_loop(0, count // 3, step, 0)
    if count % 3:
        run(count - count % 3, count % 3)


def solve(
    sizes, rows_ref, offset_ref, fields_ref, media_ref, out_ref,
    grid, nat, cross, corner, sent_rows, held_rows, chosen,
    halo_send, halo_recv, row_send, row_recv,
):
    n_sec, n_gx, n_gz = sizes
    sec, gx, gz = lax.axis_index("sec"), lax.axis_index("gx"), lax.axis_index("gz")
    is_source = sec == 0
    has_left, has_right = gx > 0, gx < n_gx - 1
    odd = lax.rem(gz, 2) == 1
    sibling = jnp.where(odd, gz - 1, gz + 1)
    lower, upper = gz == 1, gz == 2
    crossing = jnp.logical_or(lower, upper)
    partner = 3 - gz

    barrier = pltpu.get_barrier_semaphore()

    def greet(s, x, z):
        pl.semaphore_signal(barrier, inc=1, device_id=(s, x, z), device_id_type=MESH)

    cross[...] = jnp.zeros_like(cross)
    pl.when(crossing)(lambda: greet(sec, gx, partner))
    grid[...] = jnp.zeros_like(grid)
    nat[...] = jnp.zeros_like(nat)

    @pl.when(jnp.logical_not(has_right))
    def _():
        corner[0] = jnp.zeros_like(corner[0])

    @pl.when(jnp.logical_not(has_left))
    def _():
        corner[1] = jnp.zeros_like(corner[1])

    pl.when(has_left)(lambda: greet(sec, gx - 1, gz))
    pl.when(has_right)(lambda: greet(sec, gx + 1, gz))
    greet(sec, gx, sibling)

    @pl.when(is_source)
    def _():
        for s in range(1, n_sec):
            greet(s, gx, gz)

    @pl.when(jnp.logical_not(is_source))
    def _():
        greet(0, gx, gz)
        for o in range(1, n_sec - 1):
            s = 1 + lax.rem(sec - 1 + o, n_sec - 1)
            greet(s, gx, gz)
            greet(s, gx, sibling)


    for f in range(5):
        grid[f, 0, OWN:HIGH, :] = fields_ref[f].T
    for f in range(3):
        grid[5 + f, 0, OWN:HIGH, :] = media_ref[f].T

    lane1 = lax.broadcasted_iota(jnp.int32, (8, CELLS), 1)
    landing = jnp.full((8, CELLS), -1, jnp.int32)
    offset = offset_ref[jnp.maximum(sec - 1, 0)]
    for k in range(4 * NPD):
        spot = offset + lax.div(rows_ref[k], 2)
        mine = jnp.logical_and(lax.rem(lane1, 4 * NPD) == k, lane1 < 12 * NPD)
        landing = jnp.where(mine, spot, landing)
    depth = lax.broadcasted_iota(jnp.int32, (SPAN, CELLS), 0) + (gz * CELLS - REACH)
    hit = depth == jnp.broadcast_to(landing[0:1], (SPAN, CELLS))
    chosen[...] = jnp.where(hit, 0.5, 0.0).astype(jnp.bfloat16)

    waits = (
        1
        + has_left.astype(jnp.int32)
        + has_right.astype(jnp.int32)
        + crossing.astype(jnp.int32)
        + jnp.where(is_source, n_sec - 1, 1 + 2 * (n_sec - 2))
    )
    pl.semaphore_wait(barrier, waits)

    def remote(src, dst, i, where):
        return pltpu.make_async_remote_copy(
            src, dst, halo_send.at[i], halo_recv.at[i], device_id=where, device_id_type=MESH
        )

    left, right = (sec, gx - 1, gz), (sec, gx + 1, gz)
    over = (sec, gx, partner)
    near = (sec, gx, sibling)
    cross_to = pl.multiple_of(jnp.where(gz == 1, HIGH, PAD), 8)
    near_from = pl.multiple_of(jnp.where(odd, OWN, HIGH - REACH), 8)
    near_to = pl.multiple_of(jnp.where(odd, HIGH, PAD), 8)

    edge = CELLS - REACH
    left_copies = [
        remote(fields_ref.at[:, 0:REACH, :], nat.at[0:5, 0:REACH, :], 24, left),
        remote(media_ref.at[:, 0:REACH, :], nat.at[5:8, 0:REACH, :], 25, left),
    ]
    right_copies = [
        remote(fields_ref.at[:, edge:CELLS, :], nat.at[0:5, edge:CELLS, :], 26, right),
        remote(media_ref.at[:, edge:CELLS, :], nat.at[5:8, edge:CELLS, :], 27, right),
    ]

    def each(copies, name):
        def run():
            for c in copies:
                getattr(c, name)()

        return run

    deep = {0: 40, 1: 40, 2: 40, 3: 40, 4: 40, 5: 40, 6: 32, 7: 32}
    flat = {0: 32, 1: 40, 2: 40, 3: 32, 4: 32, 5: 40, 6: 32, 7: 32}

    def depths(f, act):
        if deep[f] == flat[f]:
            act(deep[f])
        else:
            pl.when(is_source)(lambda: act(deep[f]))
            pl.when(jnp.logical_not(is_source))(lambda: act(flat[f]))

    def over_copy(f, depth, low):
        if low:
            src, dst = grid.at[f, 0, HIGH - depth : HIGH, :], cross.at[f, REACH - depth : REACH, :]
        else:
            src, dst = grid.at[f, 0, OWN : OWN + depth, :], cross.at[f, 0:depth, :]
        return remote(src, dst, f, over)

    def corner_copy(f, depth, low, side):
        rows = pl.ds(0, depth) if low else pl.ds(REACH - depth, depth)
        place = left if side == 0 else right
        return remote(cross.at[f, rows, :], corner.at[side, f, rows, :], 8 + 8 * side + f, place)

    def over_start(low):
        for f in range(8):
            depths(f, lambda depth: over_copy(f, depth, low).start())

    pl.when(upper)(lambda: over_start(False))
    pl.when(lower)(lambda: over_start(True))
    pl.when(has_left)(each(left_copies, "start"))
    pl.when(has_right)(each(right_copies, "start"))


    pl.when(has_right)(each(left_copies, "wait_recv"))
    pl.when(has_left)(each(right_copies, "wait_recv"))
    for f in range(8):
        grid[f, 1, OWN:HIGH, :] = nat[f].T

    near_copy = remote(
        grid.at[:, :, pl.ds(near_from, REACH), :], grid.at[:, :, pl.ds(near_to, REACH), :], 28, near
    )
    near_copy.start()

    lanes = lax.broadcasted_iota(jnp.int32, (REACH, CELLS), 1)

    def take_halo(low):
        for f in range(8):

            def arrive(depth):
                over_copy(f, depth, not low).wait_recv()
                pl.when(has_left)(corner_copy(f, depth, low, 0).start)
                pl.when(has_right)(corner_copy(f, depth, low, 1).start)

            depths(f, arrive)
            grid[f, 0, pl.ds(cross_to, REACH), :] = cross[f]
        for f in range(8):

            def arrive(depth):
                pl.when(has_right)(corner_copy(f, depth, low, 0).wait_recv)
                pl.when(has_left)(corner_copy(f, depth, low, 1).wait_recv)

            depths(f, arrive)
            joined = jnp.where(lanes < REACH, corner[0, f], jnp.where(lanes >= edge, corner[1, f], 0.0))
            grid[f, 1, pl.ds(cross_to, REACH), :] = joined

        for f in range(8):

            def leave(depth):
                over_copy(f, depth, low).wait_send()
                pl.when(has_left)(corner_copy(f, depth, low, 0).wait_send)
                pl.when(has_right)(corner_copy(f, depth, low, 1).wait_send)

            depths(f, leave)

    pl.when(lower)(lambda: take_halo(True))
    pl.when(upper)(lambda: take_halo(False))
    near_copy.wait()

    lane = lax.broadcasted_iota(jnp.int32, (CHUNK, CELLS), 1)

    def get(f, start):
        return [grid[f, t, pl.ds(start, CHUNK), :] for t in range(2)]

    def save(start, fields):
        for f, values in fields.items():
            for t, value in enumerate(values):
                grid[f, t, pl.ds(start, CHUNK), :] = value

    def tiles(step):
        return pl.ds(0, 2 if step < STEPS - 1 else 1)

    def row_copy(i, step, where):
        return pltpu.make_async_remote_copy(
            sent_rows.at[step, tiles(step)], held_rows.at[step, tiles(step), gz], row_send.at[i, step], row_recv.at[0, step],
            device_id=where, device_id_type=MESH,
        )

    def crossed(step, part):
        return pl.ds(part, 1) if step < STEPS - 1 else pl.ds(0, 3)

    def row_over(step, s):
        parts = crossed(step, s - 1)
        return pltpu.make_async_remote_copy(
            sent_rows.at[step, tiles(step), parts], held_rows.at[step, tiles(step), gz, parts],
            row_send.at[2 + s, step], row_recv.at[2, step],
            device_id=(s, gx, partner), device_id_type=MESH,
        )

    @pl.when(is_source)
    def _():
        for step in range(STEPS):
            reach = 8 * (STEPS - step)

            def velocities(start):
                buoyancy = get(5, start)
                shear = get(4, start)
                force_x = add(along_lanes(*get(2, start), lane), along_rows(grid, 4, start))
                force_z = add(along_lanes(*shear, lane), along_rows(grid, 3, start))
                return {
                    0: [v + DT * b * g for v, b, g in zip(get(0, start), buoyancy, force_x)],
                    1: [v + DT * b * g for v, b, g in zip(get(1, start), buoyancy, force_z)],
                }

            def stresses(start):
                count = 2 if step < STEPS - 1 else 1
                first, second = get(6, start), get(7, start)
                vx, vz = get(0, start), get(1, start)
                strain_x, strain_z = along_lanes(*vx, lane), along_rows(grid, 1, start)
                bend = add(along_rows(grid, 0, start), along_lanes(*vz, lane))
                xx, zz, xz = (get(f, start)[:count] for f in (2, 3, 4))
                for t in range(count):
                    stiff = first[t] + 2.0 * second[t]
                    xx[t] = xx[t] + DT * (stiff * strain_x[t] + first[t] * strain_z[t])
                    zz[t] = zz[t] + DT * (first[t] * strain_x[t] + stiff * strain_z[t])
                    xz[t] = xz[t] + DT * second[t] * bend[t]
                return {2: xx, 3: zz, 4: xz}

            chunks(OWN - reach, HIGH + reach, velocities, save)
            chunks(OWN - reach + 8, HIGH + reach - 8, stresses, save)
            for k in range(NPD):
                row = lax.rem(rows_ref[gz * NPD + k], CELLS) + OWN
                for t in range(2):
                    line = [grid[f, t, pl.ds(row, 1), :] for f in range(4)]
                    sent_rows[step, t, 0, k : k + 1, :] = line[0]
                    sent_rows[step, t, 1, k : k + 1, :] = line[1]
                    sent_rows[step, t, 2, k : k + 1, :] = -0.5 * (line[2] + line[3])

            @pl.when(crossing)
            def _():
                for s in range(1, n_sec):
                    row_over(step, s).start()

            for s in range(1, n_sec):
                row_copy(s - 1, step, (s, gx, gz)).start()
        for step in range(STEPS):
            for s in range(1, n_sec):
                row_copy(s - 1, step, (s, gx, gz)).wait_send()
                pl.when(crossing)(row_over(step, s).wait_send)

    @pl.when(jnp.logical_not(is_source))
    def _():
        half = lax.div(gz, 2) * 2
        other = 2 - half

        part = sec - 1
        others = [lax.rem(part + 1, 3), lax.rem(part + 2, 3)]

        def hand_on(i, step, blocks, parts, where):
            piece = held_rows.at[step, tiles(step), blocks, parts]
            return pltpu.make_async_remote_copy(
                piece, piece, row_send.at[i, step], row_recv.at[i, step], device_id=where, device_id_type=MESH
            )

        whole = pl.ds(0, 3)

        def to_sibling(step):
            return hand_on(1, step, pl.ds(gz, 1), whole, near)

        def from_sibling(step):
            return hand_on(1, step, pl.ds(sibling, 1), whole, near)

        def from_partner(step):
            return hand_on(2, step, pl.ds(partner, 1), crossed(step, part), over)

        def nearby_to_partner(step):
            return hand_on(3, step, pl.ds(sibling, 1), crossed(step, part), over)

        def nearby_from_partner(step):
            return hand_on(3, step, pl.ds(3 - sibling, 1), crossed(step, part), over)

        def spread(step):
            piece = held_rows.at[step, tiles(step), pl.ds(other, 2), crossed(step, part)]
            places = [near]
            if step < STEPS - 1:
                places += [(1 + o, gx, z) for o in others for z in (gz, sibling)]
            return [
                pltpu.make_async_remote_copy(
                    piece, piece, row_send.at[i, step], row_recv.at[4 + part, step],
                    device_id=place, device_id_type=MESH,
                )
                for i, place in zip((0, 4, 5, 6, 7), places)
            ]

        def spread_in(step, which):
            parts = pl.ds(which, 1) if step < STEPS - 1 else whole
            piece = held_rows.at[step, tiles(step), pl.ds(other, 2), parts]
            return pltpu.make_async_remote_copy(
                piece, piece, row_send.at[0, step], row_recv.at[4 + which, step],
                device_id=near, device_id_type=MESH,
            )

        def velocities(start):
            buoyancy = get(5, start)
            slope_x = along_lanes(*get(2, start), lane)
            slope_z = along_rows(grid, 2, start)
            return {
                0: [v - DT * b * g for v, b, g in zip(get(0, start), buoyancy, slope_x)],
                1: [v - DT * b * g for v, b, g in zip(get(1, start), buoyancy, slope_z)],
            }

        def pressures(count, start):
            kappa, strength = get(6, start), get(7, start)
            spread = add(along_lanes(*get(0, start), lane), along_rows(grid, 1, start))
            p, one, two = (get(f, start)[:count] for f in (2, 3, 4))
            for t in range(count):
                load = kappa[t] * spread[t]
                driven = strength[t] * load
                one[t] = 0.9 * one[t] + (1.0 - 0.9) * 0.15 * driven
                two[t] = 0.5 * two[t] + (1.0 - 0.5) * 0.1 * driven
                p[t] = p[t] - DT * (load - one[t] - two[t])
            return {2: p, 3: one, 4: two}

        def evolve(step):
            reach = 8 * (STEPS - step)
            chunks(OWN - reach, HIGH + reach, velocities, save)
            count = 2 if step < STEPS - 1 else 1
            chunks(OWN - reach + 8, HIGH + reach - 8, functools.partial(pressures, count), save)

        evolve(0)

        @pl.when(crossing)
        def _():
            for step in range(STEPS):
                from_sibling(step).wait_recv()
                nearby_to_partner(step).start()

        for step in range(STEPS):
            row_copy(0, step, near).wait_recv()
            to_sibling(step).start()

        def pass_on(step):
            @pl.when(crossing)
            def _():
                nearby_from_partner(step).wait_recv()
                from_partner(step).wait_recv()
                for c in spread(step):
                    c.start()

        pass_on(0)
        for step in range(STEPS):
            if step < STEPS - 1:
                pass_on(step + 1)
            pl.when(jnp.logical_not(crossing))(from_sibling(step).wait_recv)
            for which in others if step < STEPS - 1 else []:
                spread_in(step, which).wait_recv()
            pl.when(jnp.logical_not(crossing))(spread_in(step, part).wait_recv)
            low = OWN - 8 * (STEPS - 1 - step)
            high = HIGH + 8 * (STEPS - 1 - step)
            pick = chosen[low - PAD : high - PAD, :]
            for c in range(3):
                for t in range(2 if step < STEPS - 1 else 1):
                    lines = held_rows[step, t, :, c].reshape(4 * NPD, CELLS)
                    top = lines.astype(jnp.bfloat16)
                    rest = lines - top.astype(jnp.float32)
                    mid = rest.astype(jnp.bfloat16)
                    last = (rest - mid.astype(jnp.float32)).astype(jnp.bfloat16)
                    stack = jnp.concatenate([top, mid, last, jnp.zeros_like(top)], axis=0)
                    grid[c, t, low:high, :] += jnp.dot(pick, stack, preferred_element_type=jnp.float32)
            if step < STEPS - 1:
                evolve(step + 1)

        for step in range(STEPS):
            to_sibling(step).wait_send()

            @pl.when(crossing)
            def _():
                nearby_to_partner(step).wait_send()
                for c in spread(step):
                    c.wait_send()

    for f in range(5):
        out_ref[f] = grid[f, 0, OWN:HIGH, :].T

    pl.when(has_left)(each(left_copies, "wait_send"))
    pl.when(has_right)(each(right_copies, "wait_send"))


def solution(mesh):
    sizes = tuple(mesh.shape[a] for a in ("sec", "gx", "gz"))

    def local(fields, media, plane_rows, box_offset):
        vmem = pl.BlockSpec(memory_space=pltpu.VMEM)
        smem = pl.BlockSpec(memory_space=pltpu.SMEM)
        out = pl.pallas_call(
            functools.partial(solve, sizes),
            out_shape=jax.ShapeDtypeStruct((5, CELLS, CELLS), jnp.float32),
            in_specs=[smem, smem, vmem, vmem],
            out_specs=vmem,
            scratch_shapes=[
                pltpu.VMEM((8, 2, ROWS, CELLS), jnp.float32),
                pltpu.VMEM((8, CELLS, CELLS), jnp.float32),
                pltpu.VMEM((8, REACH, CELLS), jnp.float32),
                pltpu.VMEM((2, 8, REACH, CELLS), jnp.float32),
                pltpu.VMEM((STEPS, 2, 3, NPD, CELLS), jnp.float32),
                pltpu.VMEM((STEPS, 2, 4, 3, NPD, CELLS), jnp.float32),
                pltpu.VMEM((SPAN, CELLS), jnp.bfloat16),
                pltpu.SemaphoreType.DMA((29,)),
                pltpu.SemaphoreType.DMA((29,)),
                pltpu.SemaphoreType.DMA((8, STEPS)),
                pltpu.SemaphoreType.DMA((8, STEPS)),
            ],
            compiler_params=pltpu.CompilerParams(collective_id=0, has_side_effects=True),
        )(plane_rows, box_offset, fields[0], media[0])
        return out[None]

    spec = P("sec", None, "gx", "gz")
    return jax.shard_map(
        local, mesh=mesh, in_specs=(spec, spec, P(), P()), out_specs=spec, check_vma=False
    )
```
